128 devices in a mesh: seq: 16 (over x_lo, y, core), tp: 8 (over z, x_hi).
Axes of the slice: x: 4 (x_hi: 2, x_lo: 2; x = x_hi * 2 + x_lo), y: 4, z: 4, core: 2. Of those that a mesh axis runs over, the one named last changes fastest.
Arguments:
- queries: bfloat16 [8192, 7168], P('seq', 'tp'), may hold values from -6 to 6
- new_kv: bfloat16 [2, 8192, 1024], P(None, 'seq', 'tp'), may hold values from -60 to 60, as said below
- cache_now: bfloat16 [2, 32768, 1024], P(None, 'seq', 'tp'), may hold values from -60 to 60, as said below
- cache_prev: bfloat16 [2, 2, 32768, 1024], P(None, None, 'seq', 'tp'), may hold values from -6 to 6
- out_weight: bfloat16 [7168, 7168], P('tp'), may hold values from -0.0625 to 0.0625
- residual: bfloat16 [8192, 7168], P(('seq', 'tp')), may hold values from -6 to 6
- cached_len: int32 [16], replicated, may hold values from 1 to 1536, as said below
- new_len: int32 [16], replicated, may hold values from 128 to 512, as said below
- page_table: int32 [16, 16], replicated, may hold values from -1 to 255, as said below
- dest_group: int32 [16], replicated, may hold values from 0 to 7, as said below
Outputs:
- mixed: bfloat16 [8192, 7168], P(('seq', 'tp'))
- decode_caches: bfloat16 [2, 2, 32768, 1024], P(None, None, 'seq', 'tp')
The draws below stay inside these ranges and needn't reach their ends.
Inputs may be any that keep to these rules, and one draw needn't show every extreme that they name: `cached_len`: one request has exactly 1536 cached tokens and 512 new ones. Request r's new tokens are the first new_len[r] of its 512 rows. `page_table`: entry (r, j) is device * 16 + slot of the page holding positions j * 128 to j * 128 + 127 of request r for j below ceil((cached_len[r] + new_len[r]) / 128), else -1; no page is named twice; pages j of one request with equal j // 1 lie on one device, and different such runs of one request on different devices. `dest_group`: decode group g is the seq indices 2 g and 2 g + 1; every group is named by exactly two requests. `new_kv`: keys lie within -6 to 6. `cache_now`: keys lie within -6 to 6.
All inputs are finite; a program needn't handle non-finite values.
Results may differ from the reference program's by a relative error of at most 0.013.
Values may be sent and summed in bfloat16 or wider, within the bound.
A program may use at most 128 MiB of HBM per device.

```python
import math
import jax
import jax.numpy as jnp
from jax import lax

Q_HEADS = 56
KV_HEADS = 8
HEAD_DIM = 128
MODEL_WIDTH = 7168
FRESH_ROWS = 512
SEQ_PAGES = 16
PAGE_ROWS = 128
LAYERS_MOVED = 2
REQUESTS = 16
PAGE_CAP = 1
POOL_PAGES = 16
POOL_TOTAL = 32768
HALF_ROWS = 1024
CACHE_LONGEST = 1536
N_SEQ = 16
N_TP = 8


def page_layout(key):
    layout_key = jax.random.fold_in(key, 11)
    subkeys = jax.random.split(layout_key, 5)
    cached = jax.random.randint(subkeys[0], (REQUESTS,), 1, CACHE_LONGEST + 1)
    fresh_lens = jax.random.randint(subkeys[1], (REQUESTS,), FRESH_ROWS // 4, FRESH_ROWS + 1)
    longest = jax.random.randint(subkeys[2], (), 0, REQUESTS)
    marker = jnp.arange(REQUESTS) == longest
    cached = jnp.where(marker, CACHE_LONGEST, cached).astype(jnp.int32)
    fresh_lens = jnp.where(marker, FRESH_ROWS, fresh_lens).astype(jnp.int32)
    pages_used = (cached + fresh_lens + PAGE_ROWS - 1) // PAGE_ROWS
    orders = jax.vmap(lambda subkey: jax.random.permutation(subkey, N_SEQ))(jax.random.split(subkeys[3], REQUESTS))
    slot_orders = jax.vmap(lambda subkey: jax.random.permutation(subkey, POOL_PAGES))(jax.random.split(subkeys[4], N_SEQ))
    page_ids = jnp.arange(SEQ_PAGES)
    owners = orders[:, page_ids // PAGE_CAP]
    slot_ids = slot_orders[owners, jnp.arange(REQUESTS)[:, None] * PAGE_CAP + (page_ids % PAGE_CAP)[None, :]]
    page_map = jnp.where(page_ids[None, :] < pages_used[:, None], owners * POOL_PAGES + slot_ids, -1).astype(jnp.int32)
    return (cached, fresh_lens, page_map)


def row_field(key, row_count, columns, spread, bound_value):
    sampled = jax.random.normal(key, (row_count, columns)) * spread
    return jnp.clip(sampled, -bound_value, bound_value)


def draw_queries(key, part):
    sampled = row_field(jax.random.fold_in(key, 41), REQUESTS * FRESH_ROWS, Q_HEADS * HEAD_DIM, 1.0, 6.0)
    return sampled.astype(jnp.bfloat16)


def draw_new_kv(key, part):
    key_part = row_field(jax.random.fold_in(key, 43), REQUESTS * FRESH_ROWS, KV_HEADS * HEAD_DIM, 1.0, 6.0)
    value_part = row_field(jax.random.fold_in(key, 47), REQUESTS * FRESH_ROWS, KV_HEADS * HEAD_DIM, 12.0, 60.0)
    return jnp.stack([key_part, value_part]).astype(jnp.bfloat16)


def draw_cache_now(key, part):
    key_part = row_field(jax.random.fold_in(key, 53), POOL_TOTAL, KV_HEADS * HEAD_DIM, 1.0, 6.0)
    value_part = row_field(jax.random.fold_in(key, 59), POOL_TOTAL, KV_HEADS * HEAD_DIM, 12.0, 60.0)
    return jnp.stack([key_part, value_part]).astype(jnp.bfloat16)


def draw_cached_len(key, part):
    return page_layout(key)[0]


def draw_new_len(key, part):
    return page_layout(key)[1]


def draw_page_table(key, part):
    return page_layout(key)[2]


def draw_dest_group(key, part):
    return (jax.random.permutation(jax.random.fold_in(key, 23), REQUESTS) // 2).astype(jnp.int32)


def block_levels(key, dims, cuts, least, largest):
    gain, own = 1.0, jax.random.fold_in(key, 6)
    for dim, blocks in cuts:
        draws = jnp.exp(jax.random.uniform(jax.random.fold_in(own, dim), (blocks,), jnp.float32, least / len(cuts), largest / len(cuts)))
        gain = gain * jnp.repeat(draws, dims[dim] // blocks).reshape([-1 if axis == dim else 1 for axis in range(len(dims))])
    return gain


def gaussian(stream_key, dims, scale, limit, pieces=(), kind=jnp.bfloat16):
    array = jax.random.normal(stream_key, dims, jnp.float32) * scale
    if len(pieces) > 0:
        array = block_levels(stream_key, dims, pieces, -0.22, 0.18) * array
    return jnp.clip(array, min=-limit, max=limit).astype(kind)


def setup_inputs(seed: int = 0) -> dict:
    arg_keys = jax.random.split(jax.random.key(seed), 11)
    queries = draw_queries(jax.random.fold_in(arg_keys[10], 71), 0)
    new_kv = draw_new_kv(jax.random.fold_in(arg_keys[10], 71), 0)
    cache_now = draw_cache_now(jax.random.fold_in(arg_keys[10], 71), 0)
    cache_prev = gaussian(arg_keys[3], (LAYERS_MOVED, 2, POOL_TOTAL, KV_HEADS * HEAD_DIM), 1.0, 6.0, ((2, 16), (3, 8)))
    out_weight = gaussian(arg_keys[4], (Q_HEADS * HEAD_DIM, MODEL_WIDTH), (Q_HEADS * HEAD_DIM) ** -0.5, 0.0625, ((0, 8),))
    residual = gaussian(arg_keys[5], (REQUESTS * FRESH_ROWS, MODEL_WIDTH), 1.0, 6.0, ((0, 128),))
    cached_len = draw_cached_len(jax.random.fold_in(arg_keys[10], 71), 0)
    new_len = draw_new_len(jax.random.fold_in(arg_keys[10], 71), 0)
    page_table = draw_page_table(jax.random.fold_in(arg_keys[10], 71), 0)
    dest_group = draw_dest_group(jax.random.fold_in(arg_keys[10], 71), 0)
    return dict(queries=queries, new_kv=new_kv, cache_now=cache_now, cache_prev=cache_prev, out_weight=out_weight, residual=residual, cached_len=cached_len, new_len=new_len, page_table=page_table, dest_group=dest_group)


masked_score = -1e+30

def reference(queries, new_kv, cache_now, cache_prev, out_weight, residual, cached_len, new_len, page_table, dest_group):
    group_size = Q_HEADS // KV_HEADS
    seq_rows = SEQ_PAGES * PAGE_ROWS
    score_scale = 1.0 / math.sqrt(HEAD_DIM)

    def one_request(req_index):
        cached = cached_len[req_index]
        fresh_count = new_len[req_index]
        own_table = jnp.maximum(page_table[req_index], 0)
        gather_rows = (own_table[:, None] * PAGE_ROWS + jnp.arange(PAGE_ROWS, dtype=jnp.int32)[None, :]).reshape(-1)
        cache_keys = jnp.take(cache_now[0], gather_rows, axis=0)
        cache_vals = jnp.take(cache_now[1], gather_rows, axis=0)
        first_row = (req_index * FRESH_ROWS).astype(jnp.int32)
        fresh_keys = lax.dynamic_slice_in_dim(new_kv[0], first_row, FRESH_ROWS, 0)
        fresh_vals = lax.dynamic_slice_in_dim(new_kv[1], first_row, FRESH_ROWS, 0)
        query_rows = lax.dynamic_slice_in_dim(queries, first_row, FRESH_ROWS, 0)
        positions = jnp.arange(seq_rows, dtype=jnp.int32)
        fresh_pos = cached + jnp.arange(FRESH_ROWS, dtype=jnp.int32)
        key_pos = jnp.concatenate([positions, fresh_pos])
        key_ok = jnp.concatenate([positions < cached, jnp.ones((FRESH_ROWS,), bool)])
        allowed = key_ok[None, :] & (key_pos[None, :] <= fresh_pos[:, None])
        keys_all = jnp.concatenate([cache_keys, fresh_keys]).astype(jnp.float32).reshape(-1, KV_HEADS, HEAD_DIM)
        vals_all = jnp.concatenate([cache_vals, fresh_vals]).astype(jnp.float32).reshape(-1, KV_HEADS, HEAD_DIM)
        query_all = query_rows.astype(jnp.float32).reshape(FRESH_ROWS, KV_HEADS, group_size, HEAD_DIM)
        scores = jnp.einsum('qhgd,khd->qhgk', query_all, keys_all) * score_scale
        scores = jnp.where(allowed[:, None, None, :], scores, masked_score)
        row_max = lax.optimization_barrier(jnp.max(scores, axis=-1, keepdims=True))
        weights = jnp.where(allowed[:, None, None, :], jnp.exp(scores - row_max), 0.0)
        row_total = lax.optimization_barrier(jnp.sum(weights, axis=-1))
        rounded = lax.optimization_barrier(weights.astype(jnp.bfloat16)).astype(jnp.float32)
        result = jnp.einsum('qhgk,khd->qhgd', rounded, vals_all) / row_total[..., None]
        live_rows = jnp.arange(FRESH_ROWS, dtype=jnp.int32) < fresh_count
        result = jnp.where(live_rows[:, None, None, None], result, 0.0)
        return result.reshape(FRESH_ROWS, Q_HEADS * HEAD_DIM).astype(jnp.bfloat16)
    attended = lax.map(one_request, jnp.arange(REQUESTS, dtype=jnp.int32)).reshape(REQUESTS * FRESH_ROWS, Q_HEADS * HEAD_DIM)
    head_cols = Q_HEADS * HEAD_DIM // N_TP
    mixed = residual.astype(jnp.float32)
    for group_index in range(N_TP):
        partial_value = jnp.dot(attended[:, group_index * head_cols:(group_index + 1) * head_cols], out_weight[group_index * head_cols:(group_index + 1) * head_cols], preferred_element_type=jnp.float32)
        mixed = mixed + lax.optimization_barrier(partial_value.astype(jnp.bfloat16)).astype(jnp.float32)
    mixed = mixed.astype(jnp.bfloat16)
    totals = cached_len + new_len
    request_ids = jnp.arange(REQUESTS, dtype=jnp.int32)
    same_group = dest_group[None, :] == dest_group[:, None]
    earlier = request_ids[None, :] < request_ids[:, None]
    group_rank = lax.optimization_barrier(jnp.sum((same_group & earlier).astype(jnp.int32), axis=1))
    positions = jnp.arange(seq_rows, dtype=jnp.int32)
    half_side = positions // HALF_ROWS
    source_rows = jnp.maximum(page_table, 0)[:, positions // PAGE_ROWS] * PAGE_ROWS + (positions % PAGE_ROWS)[None, :]
    target_dev = 2 * dest_group[:, None] + half_side[None, :]
    dest_rows = target_dev * seq_rows + group_rank[:, None] * HALF_ROWS + positions[None, :] - half_side[None, :] * HALF_ROWS
    valid_row = positions[None, :] < totals[:, None]
    dest_rows = jnp.where(valid_row, dest_rows, REQUESTS * seq_rows).astype(jnp.int32)
    gathered = jnp.take(cache_prev, source_rows.reshape(-1).astype(jnp.int32), axis=2)
    decoded = jnp.zeros((LAYERS_MOVED, 2, REQUESTS * seq_rows, KV_HEADS * HEAD_DIM), jnp.bfloat16)
    decoded = decoded.at[:, :, dest_rows.reshape(-1)].set(gathered, mode='drop')
    return (mixed, decoded)
```

```python
import functools
import math

import jax
import jax.numpy as jnp
from jax import lax
from jax.experimental import pallas as pl
from jax.experimental.pallas import tpu as pltpu
from jax.sharding import PartitionSpec as P

MESH = pl.DeviceIdType.MESH
BF = jnp.bfloat16
F32 = jnp.float32

N_SEQ = 16
PAGE = 128
HEADS = 7
HD = 128
FRESH = 512
CACHE_PAGES = 12
CACHE_ROWS = CACHE_PAGES * PAGE
KEYS = CACHE_ROWS + FRESH
WIDTH = 7168
GW = 512
GROUPS = WIDTH // GW
ZA = 4
XB = 3
NZ = 2 * ZA
NX = 2 * XB
CHUNK = 512
MASKED = -1e30
EXP_SCALE = math.log2(math.e) / math.sqrt(HD)
Z_STEP = (2, 1, 3, 0)


def rdma(src, dst, ssem, rsem, dev):
    return pltpu.make_async_remote_copy(
        src_ref=src, dst_ref=dst, send_sem=ssem, recv_sem=rsem, device_id=dev, device_id_type=MESH
    )


def kernel(
    tab, q_hbm, nkv_hbm, cnow_hbm, cprev_hbm, w_hbm, res_hbm,
    mixed_ref, dec_ref,
    q_v, nkv_v, cnow_v, cprev_v, w_v, res_v,
    snow, rnow, sprev, rprev, stage,
    kb, vb, qs, sbuf, att, part,
    xs, zfar, znear, xr, xfar, xnear, zxs, zxr,
    ld_sem, now_ss, now_rs, prev_ss, prev_rs, core_sem,
    zfar_ss, zfar_rs, znear_ss, znear_rs, xr_ss, xr_rs, xfar_ss, xfar_rs, xnear_ss, xnear_rs,
    zx_ss, zx_rs,
):
    s = lax.axis_index("seq")
    t = lax.axis_index("tp")
    core = s % 2
    z = t // 2
    hi = t % 2
    z_up = ((z + 1) % 4) * 2 + hi
    z_dn = ((z + 3) % 4) * 2 + hi
    up = (s, z_up)
    down = (s, z_dn)
    across = (s, z * 2 + 1 - hi)
    mate = (s + 1 - 2 * core, t)

    loads = [
        pltpu.make_async_copy(cnow_hbm, cnow_v, ld_sem.at[0]),
        pltpu.make_async_copy(cprev_hbm, cprev_v, ld_sem.at[1]),
        pltpu.make_async_copy(q_hbm, q_v, ld_sem.at[2]),
        pltpu.make_async_copy(nkv_hbm, nkv_v, ld_sem.at[3]),
        pltpu.make_async_copy(w_hbm, w_v, ld_sem.at[4]),
        pltpu.make_async_copy(res_hbm, res_v, ld_sem.at[5]),
    ]
    for copy in loads:
        copy.start()

    barrier = pltpu.get_barrier_semaphore()

    def greet(k, _):
        pl.semaphore_signal(barrier, inc=1, device_id=((s + k) % N_SEQ, t), device_id_type=MESH)
        return 0

    lax.fori_loop(1, N_SEQ, greet, 0)
    for dev in (up, down, across):
        pl.semaphore_signal(barrier, inc=1, device_id=dev, device_id_type=MESH)

    loads[0].wait()

    def pick_now(k, _):
        d = (s + k) % N_SEQ
        slot = tab[d]
        for kv in range(2):
            snow[d, kv] = cnow_v[kv, slot]
        return 0

    lax.fori_loop(1, N_SEQ, pick_now, 0)
    own_slot = tab[s]
    for kv in range(2):
        rnow[s, kv] = cnow_v[kv, own_slot]
    pl.semaphore_wait(barrier, N_SEQ - 1 + 3)

    def now_copy(src, d):
        return rdma(snow.at[d], rnow.at[src], now_ss.at[d], now_rs.at[src], (d, t))

    def send_now(k, _):
        now_copy(s, (s + k) % N_SEQ).start()
        return 0

    lax.fori_loop(1, N_SEQ, send_now, 0)

    loads[1].wait()

    def prev_copy(src, d):
        return rdma(sprev.at[d], rprev.at[src], prev_ss.at[d], prev_rs.at[src], (d, t))

    def send_prev(k, _):
        d = (s + k) % N_SEQ
        slot = tab[16 + d]
        for lk in range(4):
            sprev[d, lk] = cprev_v[lk, slot]
        prev_copy(s, d).start()
        return 0

    lax.fori_loop(1, N_SEQ, send_prev, 0)
    own_prev = tab[16 + s]
    for lk in range(4):
        rprev[s, lk] = cprev_v[lk, own_prev]

    cached = tab[64]
    fresh_count = tab[65]
    total = tab[66]
    loads[3].wait()
    loads[2].wait()
    qs[:, HD:] = jnp.ones((HEADS * PAGE, HD), BF)
    vb[:, HD:] = jnp.ones((KEYS, HD), BF)
    kb[CACHE_ROWS:, :HD] = nkv_v[0]
    vb[CACHE_ROWS:, :HD] = nkv_v[1]
    kb[CACHE_ROWS:, HD:] = jnp.zeros((FRESH, HD), BF)

    def wait_now(k, _):
        src = (s + k) % N_SEQ
        now_copy(src, src).wait_recv()
        return 0

    lax.fori_loop(1, N_SEQ, wait_now, 0)

    def place_now(j, _):
        src = tab[32 + j]
        row = pl.multiple_of(j * PAGE, PAGE)
        kb[pl.ds(row, PAGE), :HD] = rnow[src, 0]
        vb[pl.ds(row, PAGE), :HD] = rnow[src, 1]
        pos = row + lax.broadcasted_iota(jnp.int32, (PAGE, HD), 0)
        lane = lax.broadcasted_iota(jnp.int32, (PAGE, HD), 1)
        kb[pl.ds(row, PAGE), HD:] = jnp.where((lane == 0) & (pos >= cached), MASKED, 0.0).astype(BF)
        return 0

    lax.fori_loop(0, CACHE_PAGES, place_now, 0)
    loads[4].wait()
    loads[5].wait()

    def zfar_copy(side):
        half = part.at[0, ZA * side : ZA * (side + 1)]
        return rdma(half, zfar.at[side], zfar_ss.at[side], zfar_rs.at[side], (up, down)[side])

    def znear_copy(side, g):
        i = side * NZ + g
        return rdma(
            part.at[1 + side, g], znear.at[side, g], znear_ss.at[i], znear_rs.at[i], (up, down)[side]
        )

    def xr_copy(rel):
        rows = pl.ds(pl.multiple_of((1 - hi) * 64, 64), 64)
        return rdma(part.at[rel, NZ:GROUPS, rows], xr.at[rel], xr_ss.at[rel], xr_rs.at[rel], across)

    def block(rel, _):
        zb = (z + jnp.where(rel == 0, 2, jnp.where(rel == 1, 1, jnp.where(rel == 2, 3, 0)))) % 4
        row = pl.multiple_of(zb * PAGE, PAGE)
        for h in range(HEADS):
            qs[h * PAGE : (h + 1) * PAGE, :HD] = q_v[pl.ds(row, PAGE), h * HD : (h + 1) * HD]
        top = None
        for ch in range(KEYS // CHUNK):
            sc = lax.dot_general(
                qs[...], kb[ch * CHUNK : (ch + 1) * CHUNK, :], (((1,), (1,)), ((), ())),
                preferred_element_type=F32,
            )
            if ch == KEYS // CHUNK - 1:
                qpos = row + lax.broadcasted_iota(jnp.int32, (PAGE, CHUNK), 0)
                kpos = lax.broadcasted_iota(jnp.int32, (PAGE, CHUNK), 1)
                bias = jnp.where(kpos <= qpos, 0.0, MASKED)
                sc = (sc.reshape(HEADS, PAGE, CHUNK) + bias[None]).reshape(HEADS * PAGE, CHUNK)
            sbuf[:, ch * CHUNK : (ch + 1) * CHUNK] = sc
            for i in range(CHUNK // 128):
                piece = sc[:, i * 128 : (i + 1) * 128]
                top = piece if top is None else jnp.maximum(top, piece)
        peak = jnp.max(top, axis=1, keepdims=True)
        acc = None
        for ch in range(KEYS // CHUNK):
            wts = jnp.exp2((sbuf[:, ch * CHUNK : (ch + 1) * CHUNK] - peak) * EXP_SCALE).astype(BF)
            prod = jnp.dot(wts, vb[ch * CHUNK : (ch + 1) * CHUNK, :], preferred_element_type=F32)
            acc = prod if acc is None else acc + prod
        out = acc[:, :HD] / acc[:, HD:]
        live = row + lax.broadcasted_iota(jnp.int32, (PAGE, HD), 0) < fresh_count
        for h in range(HEADS):
            att[:, h * HD : (h + 1) * HD] = jnp.where(live, out[h * PAGE : (h + 1) * PAGE], 0.0).astype(BF)

        def project(g, _):
            cols = pl.ds(pl.multiple_of(g * GW, GW), GW)
            part[rel, g] = jnp.dot(att[...], w_v[:, cols], preferred_element_type=F32).astype(BF)
            return 0

        lax.fori_loop(0, GROUPS, project, 0)

        @pl.when(rel == 0)
        def _():
            zfar_copy(0).start()
            zfar_copy(1).start()

        @pl.when(rel == 1)
        def _():
            for g in range(ZA, NZ):
                znear_copy(0, g).start()

        @pl.when(rel == 2)
        def _():
            for g in range(ZA):
                znear_copy(1, g).start()

        xr_copy(rel).start()
        return 0

    lax.fori_loop(0, 4, block, 0)

    zfar_copy(0).wait_recv()
    for g in range(ZA):
        part[1, g] = (part[1, g].astype(F32) + zfar[0, g].astype(F32)).astype(BF)
        znear_copy(0, g).start()
    zfar_copy(1).wait_recv()
    for g in range(ZA):
        part[2, ZA + g] = (part[2, ZA + g].astype(F32) + zfar[1, g].astype(F32)).astype(BF)
        znear_copy(1, ZA + g).start()

    mine = pl.ds(pl.multiple_of(hi * 64, 64), 64)
    other = pl.ds(pl.multiple_of((1 - hi) * 64, 64), 64)

    def pair_sum(rel):
        xr_copy(rel).wait_recv()
        for g in range(NX):
            xs[rel, g] = (part[rel, NZ + g, mine, :].astype(F32) + xr[rel, g].astype(F32)).astype(BF)

    def xfar_copy(side):
        half = xs.at[0, XB * side : XB * (side + 1)]
        return rdma(half, xfar.at[side], xfar_ss.at[side], xfar_rs.at[side], (up, down)[side])

    def xnear_copy(side, half):
        i = side * 2 + half
        cols = pl.ds(half * XB, XB)
        return rdma(
            xs.at[1 + side, cols], xnear.at[side, cols], xnear_ss.at[i], xnear_rs.at[i], (up, down)[side]
        )

    pair_sum(0)
    xfar_copy(0).start()
    xfar_copy(1).start()
    pair_sum(1)
    xnear_copy(0, 1).start()
    pair_sum(2)
    xnear_copy(1, 0).start()

    def wait_prev(k, _):
        src = (s + k) % N_SEQ
        prev_copy(src, src).wait_recv()
        return 0

    lax.fori_loop(1, N_SEQ, wait_prev, 0)
    core_copy = rdma(stage, dec_ref.at[:, core], core_sem.at[0], core_sem.at[1], mate)

    def place_other(jj, _):
        page = (1 - core) * 8 + jj
        src = tab[48 + page]
        keep = page * PAGE + lax.broadcasted_iota(jnp.int32, (PAGE, HD), 0) < total
        for lk in range(4):
            stage[lk, jj] = jnp.where(keep, rprev[src, lk], jnp.zeros((), BF))
        return 0

    def place_own(jj, _):
        page = core * 8 + jj
        src = tab[48 + page]
        keep = page * PAGE + lax.broadcasted_iota(jnp.int32, (PAGE, HD), 0) < total
        for lk in range(4):
            dec_ref[lk, core, jj] = jnp.where(keep, rprev[src, lk], jnp.zeros((), BF))
        return 0

    lax.fori_loop(0, 8, place_other, 0)
    core_copy.start()
    lax.fori_loop(0, 8, place_own, 0)

    def zx_copy(g):
        return rdma(zxs.at[g], zxr.at[g], zx_ss.at[g], zx_rs.at[g], across)

    order = [g for pair in zip(range(ZA), range(ZA, NZ)) for g in pair]
    for g in order:
        znear_copy(0, g).wait_recv()
        znear_copy(1, g).wait_recv()
        zxs[g] = (
            part[3, g, other, :].astype(F32) + znear[0, g, other, :].astype(F32) + znear[1, g, other, :].astype(F32)
        ).astype(BF)
        zx_copy(g).start()

    xfar_copy(0).wait_recv()
    for g in range(XB):
        xs[1, g] = (xs[1, g].astype(F32) + xfar[0, g].astype(F32)).astype(BF)
    xnear_copy(0, 0).start()
    xfar_copy(1).wait_recv()
    for g in range(XB):
        xs[2, XB + g] = (xs[2, XB + g].astype(F32) + xfar[1, g].astype(F32)).astype(BF)
    xnear_copy(1, 1).start()
    xr_copy(3).wait_recv()

    for g in order:
        zx_copy(g).wait_recv()
        cols = slice(g * GW, (g + 1) * GW)
        mixed_ref[:, cols] = (
            res_v[:, cols].astype(F32)
            + part[3, g, mine, :].astype(F32)
            + znear[0, g, mine, :].astype(F32)
            + znear[1, g, mine, :].astype(F32)
            + zxr[g].astype(F32)
        ).astype(BF)
    for side in range(2):
        for half in range(2):
            xnear_copy(side, half).wait_recv()
    for g in range(NX):
        cols = slice((NZ + g) * GW, (NZ + g + 1) * GW)
        mixed_ref[:, cols] = (
            res_v[:, cols].astype(F32)
            + part[3, NZ + g, mine, :].astype(F32)
            + xr[3, g].astype(F32)
            + xnear[0, g].astype(F32)
            + xnear[1, g].astype(F32)
        ).astype(BF)

    def drain(k, _):
        d = (s + k) % N_SEQ
        now_copy(s, d).wait_send()
        prev_copy(s, d).wait_send()
        return 0

    lax.fori_loop(1, N_SEQ, drain, 0)
    for side in range(2):
        zfar_copy(side).wait_send()
        xfar_copy(side).wait_send()
        for g in range(NZ):
            znear_copy(side, g).wait_send()
        for half in range(2):
            xnear_copy(side, half).wait_send()
    for rel in range(4):
        xr_copy(rel).wait_send()
    for g in range(NZ):
        zx_copy(g).wait_send()
    core_copy.wait_send()
    rdma(stage, dec_ref.at[:, 1 - core], core_sem.at[0], core_sem.at[1], mate).wait_recv()


def tables(cached_len, new_len, page_table, dest_group):
    s = lax.axis_index("seq")
    ids = jnp.arange(16, dtype=jnp.int32)
    owner = jnp.where(page_table >= 0, page_table // 16, -1)
    slot = page_table % 16
    slot_now = jnp.sum(jnp.where(owner == s, slot, 0), axis=1)
    same = dest_group[None, :] == dest_group[:, None]
    rank = jnp.sum((same & (ids[None, :] < ids[:, None])).astype(jnp.int32), axis=1)
    dest = 2 * dest_group + rank
    slot_prev = jnp.sum(jnp.where(dest[:, None] == ids[None, :], slot_now[:, None], 0), axis=0)
    source = jnp.maximum(owner, 0)
    src_now = jnp.sum(jnp.where((ids == s)[:, None], source, 0), axis=0)
    src_prev = jnp.sum(jnp.where((dest == s)[:, None], source, 0), axis=0)
    cached = jnp.sum(jnp.where(ids == s, cached_len, 0))
    fresh = jnp.sum(jnp.where(ids == s, new_len, 0))
    total = jnp.sum(jnp.where(dest == s, cached_len + new_len, 0))
    tail = jnp.where(ids == 0, cached, jnp.where(ids == 1, fresh, jnp.where(ids == 2, total, 0)))
    return jnp.concatenate([slot_now, slot_prev, src_now, src_prev, tail]).astype(jnp.int32)


def body(
    queries, new_kv, cache_now, cache_prev, out_weight, residual, cached_len, new_len, page_table, dest_group
):
    tab = tables(cached_len, new_len, page_table, dest_group)
    any_spec = pl.BlockSpec(memory_space=pl.ANY)
    dma = pltpu.SemaphoreType.DMA
    vm = pltpu.VMEM
    mixed, decoded = pl.pallas_call(
        kernel,
        out_shape=(
            jax.ShapeDtypeStruct((64, WIDTH), BF),
            jax.ShapeDtypeStruct((4, 2, 8, PAGE, HD), BF),
        ),
        in_specs=[pl.BlockSpec(memory_space=pltpu.SMEM)] + [any_spec] * 6,
        out_specs=(pl.BlockSpec(memory_space=pltpu.VMEM), pl.BlockSpec(memory_space=pltpu.VMEM)),
        scratch_shapes=[
            vm((FRESH, HEADS * HD), BF),
            vm((2, FRESH, HD), BF),
            vm((2, 16, PAGE, HD), BF),
            vm((4, 16, PAGE, HD), BF),
            vm((HEADS * HD, WIDTH), BF),
            vm((64, WIDTH), BF),
            vm((16, 2, PAGE, HD), BF),
            vm((16, 2, PAGE, HD), BF),
            vm((16, 4, PAGE, HD), BF),
            vm((16, 4, PAGE, HD), BF),
            vm((4, 8, PAGE, HD), BF),
            vm((KEYS, 2 * HD), BF),
            vm((KEYS, 2 * HD), BF),
            vm((HEADS * PAGE, 2 * HD), BF),
            vm((HEADS * PAGE, KEYS), F32),
            vm((PAGE, HEADS * HD), BF),
            vm((4, GROUPS, PAGE, GW), BF),
            vm((3, NX, 64, GW), BF),
            vm((2, ZA, PAGE, GW), BF),
            vm((2, NZ, PAGE, GW), BF),
            vm((4, NX, 64, GW), BF),
            vm((2, XB, 64, GW), BF),
            vm((2, NX, 64, GW), BF),
            vm((NZ, 64, GW), BF),
            vm((NZ, 64, GW), BF),
            dma((6,)),
            dma((16,)), dma((16,)), dma((16,)), dma((16,)), dma((2,)),
            dma((2,)), dma((2,)), dma((2 * NZ,)), dma((2 * NZ,)), dma((4,)), dma((4,)),
            dma((2,)), dma((2,)), dma((4,)), dma((4,)), dma((NZ,)), dma((NZ,)),
        ],
        compiler_params=pltpu.CompilerParams(
            collective_id=0, has_side_effects=True, vmem_limit_bytes=66_000_000
        ),
        name="prefill",
    )(
        tab,
        queries,
        new_kv,
        cache_now.reshape(2, 16, PAGE, HD),
        cache_prev.reshape(4, 16, PAGE, HD),
        out_weight,
        residual,
    )
    return mixed, decoded.reshape(2, 2, 2048, HD)


def solution(mesh):
    placed = (
        P("seq", "tp"),
        P(None, "seq", "tp"),
        P(None, "seq", "tp"),
        P(None, None, "seq", "tp"),
        P("tp", None),
        P(("seq", "tp"), None),
        P(),
        P(),
        P(),
        P(),
    )
    return jax.shard_map(
        body,
        mesh=mesh,
        in_specs=placed,
        out_specs=(P(("seq", "tp"), None), P(None, None, "seq", "tp")),
        check_vma=False,
    )
```

```python
import functools
import math

import jax
import jax.numpy as jnp
from jax import lax
from jax.experimental import pallas as pl
from jax.experimental.pallas import tpu as pltpu
from jax.sharding import PartitionSpec as P

MESH = pl.DeviceIdType.MESH
BF = jnp.bfloat16
F32 = jnp.float32

N_SEQ = 16
PAGE = 128
HEADS = 7
HD = 128
FRESH = 512
CACHE_PAGES = 12
CACHE_ROWS = CACHE_PAGES * PAGE
KEYS = CACHE_ROWS + FRESH
WIDTH = 7168
GW = 512
GROUPS = WIDTH // GW
ZA = 5
XB = 2
NZ = 2 * ZA
NX = 2 * XB
CHUNK = 512
MASKED = -1e30
EXP_SCALE = math.log2(math.e) / math.sqrt(HD)
Z_STEP = (2, 1, 3, 0)


def rdma(src, dst, ssem, rsem, dev):
    return pltpu.make_async_remote_copy(
        src_ref=src, dst_ref=dst, send_sem=ssem, recv_sem=rsem, device_id=dev, device_id_type=MESH
    )


def kernel(
    cached_len, new_len, pages, groups, q_hbm, nkv_hbm, cnow_hbm, cprev_hbm, w_hbm, res_hbm,
    mixed_ref, dec_ref,
    q_v, nkv_v, cnow_v, cprev_v, w_v, res_v,
    snow, rnow, sprev, rprev, stage,
    kb, vb, qs, sbuf, att, part,
    xs, zfar, znear, xr, xfar, xnear, zxs, zxr,
    ld_sem, now_ss, now_rs, prev_ss, prev_rs, core_sem,
    zfar_ss, zfar_rs, znear_ss, znear_rs, xr_ss, xr_rs, xfar_ss, xfar_rs, xnear_ss, xnear_rs,
    zx_ss, zx_rs,
):
    s = lax.axis_index("seq")
    t = lax.axis_index("tp")
    core = s % 2
    z = t // 2
    hi = t % 2
    z_up = ((z + 1) % 4) * 2 + hi
    z_dn = ((z + 3) % 4) * 2 + hi
    up = (s, z_up)
    down = (s, z_dn)
    across = (s, z * 2 + 1 - hi)
    mate = (s + 1 - 2 * core, t)

    loads = [
        pltpu.make_async_copy(cnow_hbm, cnow_v, ld_sem.at[0]),
        pltpu.make_async_copy(cprev_hbm, cprev_v, ld_sem.at[1]),
        pltpu.make_async_copy(q_hbm, q_v, ld_sem.at[2]),
        pltpu.make_async_copy(nkv_hbm, nkv_v, ld_sem.at[3]),
        pltpu.make_async_copy(w_hbm, w_v, ld_sem.at[4]),
        pltpu.make_async_copy(res_hbm, res_v, ld_sem.at[5]),
    ]
    loads[0].start()
    loads[1].start()

    barrier = pltpu.get_barrier_semaphore()

    def greet(k, _):
        pl.semaphore_signal(barrier, inc=1, device_id=((s + k) % N_SEQ, t), device_id_type=MESH)
        return 0

    lax.fori_loop(1, N_SEQ, greet, 0)
    for dev in (up, down, across):
        pl.semaphore_signal(barrier, inc=1, device_id=dev, device_id_type=MESH)

    def slot_of(r):
        slot = 0
        for j in range(16):
            entry = pages[r, j]
            slot = jnp.where((entry >> 4) == s, entry & 15, slot)
        return slot

    def request_at(d):
        first = 15
        last = 0
        for r in range(16):
            mine = groups[r] == d // 2
            first = jnp.minimum(first, jnp.where(mine, r, 15))
            last = jnp.maximum(last, jnp.where(mine, r, 0))
        return jnp.where(d % 2 == 0, first, last)

    loads[0].wait()
    for copy in loads[2:]:
        copy.start()

    def pick_now(k, _):
        d = (s + k) % N_SEQ
        slot = slot_of(d)
        for kv in range(2):
            snow[d, kv] = cnow_v[kv, slot]
        return 0

    lax.fori_loop(1, N_SEQ, pick_now, 0)
    own_slot = slot_of(s)
    for kv in range(2):
        rnow[s, kv] = cnow_v[kv, own_slot]
    pl.semaphore_wait(barrier, N_SEQ - 1 + 3)

    def now_copy(src, d):
        return rdma(snow.at[d], rnow.at[src], now_ss.at[d], now_rs.at[src], (d, t))

    def send_now(k, _):
        now_copy(s, (s + k) % N_SEQ).start()
        return 0

    lax.fori_loop(1, N_SEQ, send_now, 0)

    loads[1].wait()

    def prev_copy(src, d):
        return rdma(sprev.at[d], rprev.at[src], prev_ss.at[d], prev_rs.at[src], (d, t))

    def send_prev(k, _):
        d = (s + k) % N_SEQ
        slot = slot_of(request_at(d))
        for lk in range(4):
            sprev[d, lk] = cprev_v[lk, slot]
        prev_copy(s, d).start()
        return 0

    lax.fori_loop(1, N_SEQ, send_prev, 0)
    moved = request_at(s)
    own_prev = slot_of(moved)
    for lk in range(4):
        rprev[s, lk] = cprev_v[lk, own_prev]

    cached = cached_len[s]
    fresh_count = new_len[s]
    total = cached_len[moved] + new_len[moved]
    loads[3].wait()
    loads[2].wait()
    qs[:, HD:] = jnp.ones((HEADS * PAGE, HD), BF)
    vb[:, HD:] = jnp.ones((KEYS, HD), BF)
    kb[CACHE_ROWS:, :HD] = nkv_v[0]
    vb[CACHE_ROWS:, :HD] = nkv_v[1]
    kb[CACHE_ROWS:, HD:] = jnp.zeros((FRESH, HD), BF)

    def wait_now(k, _):
        src = (s + k) % N_SEQ
        now_copy(src, src).wait_recv()
        return 0

    lax.fori_loop(1, N_SEQ, wait_now, 0)

    def place_now(j, _):
        src = jnp.maximum(pages[s, j] >> 4, 0)
        row = pl.multiple_of(j * PAGE, PAGE)
        kb[pl.ds(row, PAGE), :HD] = rnow[src, 0]
        vb[pl.ds(row, PAGE), :HD] = rnow[src, 1]
        pos = row + lax.broadcasted_iota(jnp.int32, (PAGE, HD), 0)
        lane = lax.broadcasted_iota(jnp.int32, (PAGE, HD), 1)
        kb[pl.ds(row, PAGE), HD:] = jnp.where((lane == 0) & (pos >= cached), MASKED, 0.0).astype(BF)
        return 0

    lax.fori_loop(0, CACHE_PAGES, place_now, 0)
    loads[4].wait()
    loads[5].wait()

    def zfar_copy(side):
        half = part.at[0, ZA * side : ZA * (side + 1)]
        return rdma(half, zfar.at[side], zfar_ss.at[side], zfar_rs.at[side], (up, down)[side])

    def znear_copy(side, g):
        i = side * NZ + g
        return rdma(
            part.at[1 + side, g], znear.at[side, g], znear_ss.at[i], znear_rs.at[i], (up, down)[side]
        )

    def xr_copy(rel):
        rows = pl.ds(pl.multiple_of((1 - hi) * 64, 64), 64)
        return rdma(part.at[rel, NZ:GROUPS, rows], xr.at[rel], xr_ss.at[rel], xr_rs.at[rel], across)

    def block(rel, _):
        @pl.when(rel == 3)
        def _():
            zfar_copy(0).wait_recv()
            for g in range(ZA):
                part[1, g] = (part[1, g].astype(F32) + zfar[0, g].astype(F32)).astype(BF)
                znear_copy(0, g).start()
            zfar_copy(1).wait_recv()
            for g in range(ZA):
                part[2, ZA + g] = (part[2, ZA + g].astype(F32) + zfar[1, g].astype(F32)).astype(BF)
                znear_copy(1, ZA + g).start()

        zb = (z + jnp.where(rel == 0, 2, jnp.where(rel == 1, 1, jnp.where(rel == 2, 3, 0)))) % 4
        row = pl.multiple_of(zb * PAGE, PAGE)
        for h in range(HEADS):
            qs[h * PAGE : (h + 1) * PAGE, :HD] = q_v[pl.ds(row, PAGE), h * HD : (h + 1) * HD]
        top = None
        for ch in range(KEYS // CHUNK):
            sc = lax.dot_general(
                qs[...], kb[ch * CHUNK : (ch + 1) * CHUNK, :], (((1,), (1,)), ((), ())),
                preferred_element_type=F32,
            )
            if ch == KEYS // CHUNK - 1:
                qpos = row + lax.broadcasted_iota(jnp.int32, (PAGE, CHUNK), 0)
                kpos = lax.broadcasted_iota(jnp.int32, (PAGE, CHUNK), 1)
                bias = jnp.where(kpos <= qpos, 0.0, MASKED)
                sc = (sc.reshape(HEADS, PAGE, CHUNK) + bias[None]).reshape(HEADS * PAGE, CHUNK)
            sbuf[:, ch * CHUNK : (ch + 1) * CHUNK] = sc
            for i in range(CHUNK // 128):
                piece = sc[:, i * 128 : (i + 1) * 128]
                top = piece if top is None else jnp.maximum(top, piece)
        peak = jnp.max(top, axis=1, keepdims=True)
        acc = None
        for ch in range(KEYS // CHUNK):
            wts = jnp.exp2((sbuf[:, ch * CHUNK : (ch + 1) * CHUNK] - peak) * EXP_SCALE).astype(BF)
            prod = jnp.dot(wts, vb[ch * CHUNK : (ch + 1) * CHUNK, :], preferred_element_type=F32)
            acc = prod if acc is None else acc + prod
        out = acc[:, :HD] / acc[:, HD:]
        live = row + lax.broadcasted_iota(jnp.int32, (PAGE, HD), 0) < fresh_count
        for h in range(HEADS):
            att[:, h * HD : (h + 1) * HD] = jnp.where(live, out[h * PAGE : (h + 1) * PAGE], 0.0).astype(BF)

        def project(g, _):
            cols = pl.ds(pl.multiple_of(g * GW, GW), GW)
            part[rel, g] = jnp.dot(att[...], w_v[:, cols], preferred_element_type=F32).astype(BF)
            return 0

        lax.fori_loop(0, GROUPS, project, 0)

        @pl.when(rel == 0)
        def _():
            zfar_copy(0).start()
            zfar_copy(1).start()

        @pl.when(rel == 1)
        def _():
            for g in range(ZA, NZ):
                znear_copy(0, g).start()

        @pl.when(rel == 2)
        def _():
            for g in range(ZA):
                znear_copy(1, g).start()

        xr_copy(rel).start()
        return 0

    lax.fori_loop(0, 4, block, 0)

    mine = pl.ds(pl.multiple_of(hi * 64, 64), 64)
    other = pl.ds(pl.multiple_of((1 - hi) * 64, 64), 64)

    def pair_sum(rel):
        xr_copy(rel).wait_recv()
        for g in range(NX):
            xs[rel, g] = (part[rel, NZ + g, mine, :].astype(F32) + xr[rel, g].astype(F32)).astype(BF)

    def xfar_copy(side):
        half = xs.at[0, XB * side : XB * (side + 1)]
        return rdma(half, xfar.at[side], xfar_ss.at[side], xfar_rs.at[side], (up, down)[side])

    def xnear_copy(side, half):
        i = side * 2 + half
        cols = pl.ds(half * XB, XB)
        return rdma(
            xs.at[1 + side, cols], xnear.at[side, cols], xnear_ss.at[i], xnear_rs.at[i], (up, down)[side]
        )

    pair_sum(0)
    xfar_copy(0).start()
    xfar_copy(1).start()
    pair_sum(1)
    xnear_copy(0, 1).start()
    pair_sum(2)
    xnear_copy(1, 0).start()

    def wait_prev(k, _):
        src = (s + k) % N_SEQ
        prev_copy(src, src).wait_recv()
        return 0

    lax.fori_loop(1, N_SEQ, wait_prev, 0)
    core_copy = rdma(stage, dec_ref.at[:, core], core_sem.at[0], core_sem.at[1], mate)

    def place_other(jj, _):
        page = (1 - core) * 8 + jj
        src = jnp.maximum(pages[moved, page] >> 4, 0)
        keep = page * PAGE + lax.broadcasted_iota(jnp.int32, (PAGE, HD), 0) < total
        for lk in range(4):
            stage[lk, jj] = jnp.where(keep, rprev[src, lk], jnp.zeros((), BF))
        return 0

    def place_own(jj, _):
        page = core * 8 + jj
        src = jnp.maximum(pages[moved, page] >> 4, 0)
        keep = page * PAGE + lax.broadcasted_iota(jnp.int32, (PAGE, HD), 0) < total
        for lk in range(4):
            dec_ref[lk, core, jj] = jnp.where(keep, rprev[src, lk], jnp.zeros((), BF))
        return 0

    lax.fori_loop(0, 8, place_other, 0)
    core_copy.start()
    lax.fori_loop(0, 8, place_own, 0)

    def zx_copy(g):
        return rdma(zxs.at[g], zxr.at[g], zx_ss.at[g], zx_rs.at[g], across)

    order = [g for pair in zip(range(ZA), range(ZA, NZ)) for g in pair]
    for g in order:
        znear_copy(0, g).wait_recv()
        znear_copy(1, g).wait_recv()
        zxs[g] = (
            part[3, g, other, :].astype(F32) + znear[0, g, other, :].astype(F32) + znear[1, g, other, :].astype(F32)
        ).astype(BF)
        zx_copy(g).start()

    xfar_copy(0).wait_recv()
    for g in range(XB):
        xs[1, g] = (xs[1, g].astype(F32) + xfar[0, g].astype(F32)).astype(BF)
    xnear_copy(0, 0).start()
    xfar_copy(1).wait_recv()
    for g in range(XB):
        xs[2, XB + g] = (xs[2, XB + g].astype(F32) + xfar[1, g].astype(F32)).astype(BF)
    xnear_copy(1, 1).start()
    xr_copy(3).wait_recv()

    for g in order:
        zx_copy(g).wait_recv()
        cols = slice(g * GW, (g + 1) * GW)
        mixed_ref[:, cols] = (
            res_v[:, cols].astype(F32)
            + part[3, g, mine, :].astype(F32)
            + znear[0, g, mine, :].astype(F32)
            + znear[1, g, mine, :].astype(F32)
            + zxr[g].astype(F32)
        ).astype(BF)
    for side in range(2):
        for half in range(2):
            xnear_copy(side, half).wait_recv()
    for g in range(NX):
        cols = slice((NZ + g) * GW, (NZ + g + 1) * GW)
        mixed_ref[:, cols] = (
            res_v[:, cols].astype(F32)
            + part[3, NZ + g, mine, :].astype(F32)
            + xr[3, g].astype(F32)
            + xnear[0, g].astype(F32)
            + xnear[1, g].astype(F32)
        ).astype(BF)

    def drain(k, _):
        d = (s + k) % N_SEQ
        now_copy(s, d).wait_send()
        prev_copy(s, d).wait_send()
        return 0

    lax.fori_loop(1, N_SEQ, drain, 0)
    for side in range(2):
        zfar_copy(side).wait_send()
        xfar_copy(side).wait_send()
        for g in range(NZ):
            znear_copy(side, g).wait_send()
        for half in range(2):
            xnear_copy(side, half).wait_send()
    for rel in range(4):
        xr_copy(rel).wait_send()
    for g in range(NZ):
        zx_copy(g).wait_send()
    core_copy.wait_send()
    rdma(stage, dec_ref.at[:, 1 - core], core_sem.at[0], core_sem.at[1], mate).wait_recv()


def body(
    queries, new_kv, cache_now, cache_prev, out_weight, residual, cached_len, new_len, page_table, dest_group
):
    any_spec = pl.BlockSpec(memory_space=pl.ANY)
    dma = pltpu.SemaphoreType.DMA
    vm = pltpu.VMEM
    mixed, decoded = pl.pallas_call(
        kernel,
        out_shape=(
            jax.ShapeDtypeStruct((64, WIDTH), BF),
            jax.ShapeDtypeStruct((4, 2, 8, PAGE, HD), BF),
        ),
        in_specs=[pl.BlockSpec(memory_space=pltpu.SMEM)] * 4 + [any_spec] * 6,
        out_specs=(pl.BlockSpec(memory_space=pltpu.VMEM), pl.BlockSpec(memory_space=pltpu.VMEM)),
        scratch_shapes=[
            vm((FRESH, HEADS * HD), BF),
            vm((2, FRESH, HD), BF),
            vm((2, 16, PAGE, HD), BF),
            vm((4, 16, PAGE, HD), BF),
            vm((HEADS * HD, WIDTH), BF),
            vm((64, WIDTH), BF),
            vm((16, 2, PAGE, HD), BF),
            vm((16, 2, PAGE, HD), BF),
            vm((16, 4, PAGE, HD), BF),
            vm((16, 4, PAGE, HD), BF),
            vm((4, 8, PAGE, HD), BF),
            vm((KEYS, 2 * HD), BF),
            vm((KEYS, 2 * HD), BF),
            vm((HEADS * PAGE, 2 * HD), BF),
            vm((HEADS * PAGE, KEYS), F32),
            vm((PAGE, HEADS * HD), BF),
            vm((4, GROUPS, PAGE, GW), BF),
            vm((3, NX, 64, GW), BF),
            vm((2, ZA, PAGE, GW), BF),
            vm((2, NZ, PAGE, GW), BF),
            vm((4, NX, 64, GW), BF),
            vm((2, XB, 64, GW), BF),
            vm((2, NX, 64, GW), BF),
            vm((NZ, 64, GW), BF),
            vm((NZ, 64, GW), BF),
            dma((6,)),
            dma((16,)), dma((16,)), dma((16,)), dma((16,)), dma((2,)),
            dma((2,)), dma((2,)), dma((2 * NZ,)), dma((2 * NZ,)), dma((4,)), dma((4,)),
            dma((2,)), dma((2,)), dma((4,)), dma((4,)), dma((NZ,)), dma((NZ,)),
        ],
        compiler_params=pltpu.CompilerParams(
            collective_id=0, has_side_effects=True, vmem_limit_bytes=66_000_000
        ),
        name="prefill",
    )(
        cached_len,
        new_len,
        page_table,
        dest_group,
        queries,
        new_kv,
        cache_now.reshape(2, 16, PAGE, HD),
        cache_prev.reshape(4, 16, PAGE, HD),
        out_weight,
        residual,
    )
    return mixed, decoded.reshape(2, 2, 2048, HD)


def solution(mesh):
    placed = (
        P("seq", "tp"),
        P(None, "seq", "tp"),
        P(None, "seq", "tp"),
        P(None, None, "seq", "tp"),
        P("tp", None),
        P(("seq", "tp"), None),
        P(),
        P(),
        P(),
        P(),
    )
    return jax.shard_map(
        body,
        mesh=mesh,
        in_specs=placed,
        out_specs=(P(("seq", "tp"), None), P(None, None, "seq", "tp")),
        check_vma=False,
    )
```

```python
import functools
import math

import jax
import jax.numpy as jnp
from jax import lax
from jax.experimental import pallas as pl
from jax.experimental.pallas import tpu as pltpu
from jax.sharding import PartitionSpec as P

MESH = pl.DeviceIdType.MESH
BF = jnp.bfloat16
F32 = jnp.float32

N_SEQ = 16
PAGE = 128
HEADS = 7
HD = 128
FRESH = 512
CACHE_PAGES = 12
CACHE_ROWS = CACHE_PAGES * PAGE
KEYS = CACHE_ROWS + FRESH
WIDTH = 7168
GW = 512
GROUPS = WIDTH // GW
ZA = 5
XB = 2
NZ = 2 * ZA
NX = 2 * XB
CHUNK = 512
MASKED = -1e30
EXP_SCALE = math.log2(math.e) / math.sqrt(HD)


def rdma(src, dst, ssem, rsem, dev):
    return pltpu.make_async_remote_copy(
        src_ref=src, dst_ref=dst, send_sem=ssem, recv_sem=rsem, device_id=dev, device_id_type=MESH
    )


def kernel(
    cached_len, new_len, pages, groups, q_hbm, nkv_hbm, cnow_hbm, cprev_hbm, w_hbm, res_hbm,
    mixed_ref, dec_ref,
    q_v, nkv_v, cnow_v, cprev_v, w_v, res_v,
    snow, rnow, sprev, rprev, stage,
    kb, vb, qs, sbuf, att, part,
    xs, zfar, znear, xr, xrn, xfar, xnear, zxs, zxr,
    ld_sem, now_ss, now_rs, prev_ss, prev_rs, core_sem,
    zfar_ss, zfar_rs, znear_ss, znear_rs, xr_ss, xr_rs, xfar_ss, xfar_rs, xnear_ss, xnear_rs,
    zx_ss, zx_rs,
):
    s = lax.axis_index("seq")
    t = lax.axis_index("tp")
    core = s % 2
    z = t // 2
    hi = t % 2
    z_up = ((z + 1) % 4) * 2 + hi
    z_dn = ((z + 3) % 4) * 2 + hi
    up = (s, z_up)
    down = (s, z_dn)
    across = (s, z * 2 + 1 - hi)
    mate = (s + 1 - 2 * core, t)

    loads = [
        pltpu.make_async_copy(cnow_hbm, cnow_v, ld_sem.at[0]),
        pltpu.make_async_copy(cprev_hbm, cprev_v, ld_sem.at[1]),
        pltpu.make_async_copy(q_hbm, q_v, ld_sem.at[2]),
        pltpu.make_async_copy(nkv_hbm, nkv_v, ld_sem.at[3]),
        pltpu.make_async_copy(w_hbm, w_v, ld_sem.at[4]),
        pltpu.make_async_copy(res_hbm, res_v, ld_sem.at[5]),
    ]
    loads[0].start()
    loads[1].start()

    barrier = pltpu.get_barrier_semaphore()

    def greet(k, _):
        pl.semaphore_signal(barrier, inc=1, device_id=((s + k) % N_SEQ, t), device_id_type=MESH)
        return 0

    lax.fori_loop(1, N_SEQ, greet, 0)
    for dev in (up, down, across):
        pl.semaphore_signal(barrier, inc=1, device_id=dev, device_id_type=MESH)

    def slot_of(r):
        slot = 0
        for j in range(16):
            entry = pages[r, j]
            slot = jnp.where((entry >> 4) == s, entry & 15, slot)
        return slot

    def request_at(d):
        first = 15
        last = 0
        for r in range(16):
            mine = groups[r] == d // 2
            first = jnp.minimum(first, jnp.where(mine, r, 15))
            last = jnp.maximum(last, jnp.where(mine, r, 0))
        return jnp.where(d % 2 == 0, first, last)

    loads[0].wait()
    for copy in loads[2:]:
        copy.start()

    def pick_now(k, _):
        d = (s + k) % N_SEQ
        slot = slot_of(d)
        for kv in range(2):
            snow[d, kv] = cnow_v[kv, slot]
        return 0

    lax.fori_loop(1, N_SEQ, pick_now, 0)
    own_slot = slot_of(s)
    for kv in range(2):
        rnow[s, kv] = cnow_v[kv, own_slot]
    pl.semaphore_wait(barrier, N_SEQ - 1 + 3)

    def now_copy(src, d):
        return rdma(snow.at[d], rnow.at[src], now_ss.at[d], now_rs.at[src], (d, t))

    def send_now(k, _):
        now_copy(s, (s + k) % N_SEQ).start()
        return 0

    lax.fori_loop(1, N_SEQ, send_now, 0)

    loads[1].wait()

    def prev_copy(src, d):
        return rdma(sprev.at[d], rprev.at[src], prev_ss.at[d], prev_rs.at[src], (d, t))

    def send_prev(k, _):
        d = (s + k) % N_SEQ
        slot = slot_of(request_at(d))
        for lk in range(4):
            sprev[d, lk] = cprev_v[lk, slot]
        prev_copy(s, d).start()
        return 0

    lax.fori_loop(1, N_SEQ, send_prev, 0)
    moved = request_at(s)
    own_prev = slot_of(moved)
    for lk in range(4):
        rprev[s, lk] = cprev_v[lk, own_prev]

    cached = cached_len[s]
    fresh_count = new_len[s]
    total = cached_len[moved] + new_len[moved]
    loads[3].wait()
    loads[2].wait()
    qs[:, HD:] = jnp.ones((HEADS * PAGE, HD), BF)
    vb[:, HD:] = jnp.ones((KEYS, HD), BF)
    kb[CACHE_ROWS:, :HD] = nkv_v[0]
    vb[CACHE_ROWS:, :HD] = nkv_v[1]
    kb[CACHE_ROWS:, HD:] = jnp.zeros((FRESH, HD), BF)

    def wait_now(k, _):
        src = (s + k) % N_SEQ
        now_copy(src, src).wait_recv()
        return 0

    lax.fori_loop(1, N_SEQ, wait_now, 0)

    def place_now(j, _):
        src = jnp.maximum(pages[s, j] >> 4, 0)
        row = pl.multiple_of(j * PAGE, PAGE)
        kb[pl.ds(row, PAGE), :HD] = rnow[src, 0]
        vb[pl.ds(row, PAGE), :HD] = rnow[src, 1]
        pos = row + lax.broadcasted_iota(jnp.int32, (PAGE, HD), 0)
        lane = lax.broadcasted_iota(jnp.int32, (PAGE, HD), 1)
        kb[pl.ds(row, PAGE), HD:] = jnp.where((lane == 0) & (pos >= cached), MASKED, 0.0).astype(BF)
        return 0

    lax.fori_loop(0, CACHE_PAGES, place_now, 0)
    loads[4].wait()
    loads[5].wait()

    mine = pl.ds(pl.multiple_of(hi * 64, 64), 64)
    other = pl.ds(pl.multiple_of((1 - hi) * 64, 64), 64)

    def zfar_copy(side, i):
        k = side * ZA + i
        return rdma(part.at[0, k], zfar.at[side, i], zfar_ss.at[k], zfar_rs.at[k], (up, down)[side])

    def znear_copy(side, g, half):
        i = (side * NZ + g) * 2 + half
        return rdma(
            part.at[1 + half, g, side * 64 : (side + 1) * 64],
            znear.at[side, g, half * 64 : (half + 1) * 64],
            znear_ss.at[i], znear_rs.at[i], (up, down)[side],
        )

    def xr_copy(part_of):
        if part_of == 1:
            return rdma(part.at[1, NZ:GROUPS], xrn, xr_ss.at[1], xr_rs.at[1], across)
        src = part.at[3 * part_of // 2, NZ:GROUPS, other]
        return rdma(src, xr.at[part_of // 2], xr_ss.at[part_of], xr_rs.at[part_of], across)

    def pass_on(half):
        rows = (other, mine)[half]
        for i in range(ZA):
            for side in range(2):
                g = side * ZA + i
                cut = slice(side * 64, (side + 1) * 64)
                part[1 + half, g, cut, :] = (
                    part[1 + half, g, cut, :].astype(F32) + zfar[side, i, rows, :].astype(F32)
                ).astype(BF)
                znear_copy(side, g, half).start()

    def block(rel, _):
        near = (rel == 1) | (rel == 2)
        part_row = jnp.where(rel == 1, 1 - hi, hi) * 64
        above = ((z + 1) % 4) * PAGE + part_row
        below = ((z + 3) % 4) * PAGE + part_row
        whole = jnp.where(rel == 0, (z + 2) % 4, z) * PAGE
        row_a = pl.multiple_of(jnp.where(near, above, whole), 64)
        row_b = pl.multiple_of(jnp.where(near, below, whole + 64), 64)
        for h in range(HEADS):
            qs[h * PAGE : h * PAGE + 64, :HD] = q_v[pl.ds(row_a, 64), h * HD : (h + 1) * HD]
            qs[h * PAGE + 64 : (h + 1) * PAGE, :HD] = q_v[pl.ds(row_b, 64), h * HD : (h + 1) * HD]

        def position(shape):
            r = lax.broadcasted_iota(jnp.int32, shape, 0)
            return r + jnp.where(r < 64, row_a, row_b - 64)

        top = None
        for ch in range(KEYS // CHUNK):
            sc = lax.dot_general(
                qs[...], kb[ch * CHUNK : (ch + 1) * CHUNK, :], (((1,), (1,)), ((), ())),
                preferred_element_type=F32,
            )
            if ch == KEYS // CHUNK - 1:
                qpos = position((PAGE, CHUNK))
                kpos = lax.broadcasted_iota(jnp.int32, (PAGE, CHUNK), 1)
                bias = jnp.where(kpos <= qpos, 0.0, MASKED)
                sc = (sc.reshape(HEADS, PAGE, CHUNK) + bias[None]).reshape(HEADS * PAGE, CHUNK)
            sbuf[:, ch * CHUNK : (ch + 1) * CHUNK] = sc
            for i in range(CHUNK // 128):
                piece = sc[:, i * 128 : (i + 1) * 128]
                top = piece if top is None else jnp.maximum(top, piece)
        peak = jnp.max(top, axis=1, keepdims=True)
        acc = None
        for ch in range(KEYS // CHUNK):
            wts = jnp.exp2((sbuf[:, ch * CHUNK : (ch + 1) * CHUNK] - peak) * EXP_SCALE).astype(BF)
            prod = jnp.dot(wts, vb[ch * CHUNK : (ch + 1) * CHUNK, :], preferred_element_type=F32)
            acc = prod if acc is None else acc + prod
        out = acc[:, :HD] / acc[:, HD:]
        live = position((PAGE, HD)) < fresh_count
        for h in range(HEADS):
            att[:, h * HD : (h + 1) * HD] = jnp.where(live, out[h * PAGE : (h + 1) * PAGE], 0.0).astype(BF)

        @pl.when(rel == 2)
        def _():
            for side in range(2):
                for i in range(ZA):
                    zfar_copy(side, i).wait_recv()
            pass_on(0)

        def project(g):
            cols = pl.ds(pl.multiple_of(g * GW, GW), GW)
            part[rel, g] = jnp.dot(att[...], w_v[:, cols], preferred_element_type=F32).astype(BF)

        def z_first(i, _):
            for side in range(2):
                project(side * ZA + i)

                @pl.when(rel == 0)
                def _():
                    zfar_copy(side, i).start()

            return 0

        def x_first(g, _):
            project(g)
            return 0

        lax.fori_loop(0, ZA, z_first, 0)

        for half in range(2):

            @pl.when(rel == 1 + half)
            def _():
                for i in range(ZA):
                    znear_copy(0, ZA + i, half).start()
                    znear_copy(1, i, half).start()

        lax.fori_loop(NZ, GROUPS, x_first, 0)
        for part_of in range(3):

            @pl.when(rel == (0, 1, 3)[part_of])
            def _():
                xr_copy(part_of).start()

        @pl.when(rel == 2)
        def _():
            pass_on(1)

        return 0

    lax.fori_loop(0, 4, block, 0)

    def pair_sum(rel):
        for g in range(NX):
            if rel == 0:
                own, got = part[0, NZ + g, mine, :], xr[0, g]
            else:
                cut = slice((rel - 1) * 64, rel * 64)
                own, got = part[2, NZ + g, cut, :], xrn[g, cut]
            xs[rel, g] = (own.astype(F32) + got.astype(F32)).astype(BF)

    def xfar_copy(side):
        half = xs.at[0, XB * side : XB * (side + 1)]
        return rdma(half, xfar.at[side], xfar_ss.at[side], xfar_rs.at[side], (up, down)[side])

    def xnear_copy(side, half):
        i = side * 2 + half
        cols = pl.ds(half * XB, XB)
        return rdma(
            xs.at[1 + side, cols], xnear.at[side, cols], xnear_ss.at[i], xnear_rs.at[i], (up, down)[side]
        )

    xr_copy(0).wait_recv()
    pair_sum(0)
    xfar_copy(0).start()
    xfar_copy(1).start()
    xr_copy(1).wait_recv()
    pair_sum(1)
    xnear_copy(0, 1).start()
    pair_sum(2)
    xnear_copy(1, 0).start()

    def wait_prev(k, _):
        src = (s + k) % N_SEQ
        prev_copy(src, src).wait_recv()
        return 0

    lax.fori_loop(1, N_SEQ, wait_prev, 0)
    core_copy = rdma(stage, dec_ref.at[:, core], core_sem.at[0], core_sem.at[1], mate)

    def place_other(jj, _):
        page = (1 - core) * 8 + jj
        src = jnp.maximum(pages[moved, page] >> 4, 0)
        keep = page * PAGE + lax.broadcasted_iota(jnp.int32, (PAGE, HD), 0) < total
        for lk in range(4):
            stage[lk, jj] = jnp.where(keep, rprev[src, lk], jnp.zeros((), BF))
        return 0

    def place_own(jj, _):
        page = core * 8 + jj
        src = jnp.maximum(pages[moved, page] >> 4, 0)
        keep = page * PAGE + lax.broadcasted_iota(jnp.int32, (PAGE, HD), 0) < total
        for lk in range(4):
            dec_ref[lk, core, jj] = jnp.where(keep, rprev[src, lk], jnp.zeros((), BF))
        return 0

    lax.fori_loop(0, 8, place_other, 0)
    core_copy.start()
    lax.fori_loop(0, 8, place_own, 0)

    def zx_copy(g):
        return rdma(zxs.at[g], zxr.at[g], zx_ss.at[g], zx_rs.at[g], across)

    order = [g for pair in zip(range(ZA), range(ZA, NZ)) for g in pair]
    for g in order:
        znear_copy(0, g, 0).wait_recv()
        znear_copy(1, g, 0).wait_recv()
        zxs[g] = (
            part[3, g, other, :].astype(F32) + znear[0, g, :64].astype(F32) + znear[1, g, :64].astype(F32)
        ).astype(BF)
        zx_copy(g).start()

    xfar_copy(0).wait_recv()
    for g in range(XB):
        xs[1, g] = (xs[1, g].astype(F32) + xfar[0, g].astype(F32)).astype(BF)
    xnear_copy(0, 0).start()
    xfar_copy(1).wait_recv()
    for g in range(XB):
        xs[2, XB + g] = (xs[2, XB + g].astype(F32) + xfar[1, g].astype(F32)).astype(BF)
    xnear_copy(1, 1).start()
    xr_copy(2).wait_recv()

    for g in order:
        zx_copy(g).wait_recv()
        znear_copy(0, g, 1).wait_recv()
        znear_copy(1, g, 1).wait_recv()
        cols = slice(g * GW, (g + 1) * GW)
        mixed_ref[:, cols] = (
            res_v[:, cols].astype(F32)
            + part[3, g, mine, :].astype(F32)
            + znear[0, g, 64:].astype(F32)
            + znear[1, g, 64:].astype(F32)
            + zxr[g].astype(F32)
        ).astype(BF)
    for side in range(2):
        for half in range(2):
            xnear_copy(side, half).wait_recv()
    for g in range(NX):
        cols = slice((NZ + g) * GW, (NZ + g + 1) * GW)
        mixed_ref[:, cols] = (
            res_v[:, cols].astype(F32)
            + part[3, NZ + g, mine, :].astype(F32)
            + xr[1, g].astype(F32)
            + xnear[0, g].astype(F32)
            + xnear[1, g].astype(F32)
        ).astype(BF)

    def drain(k, _):
        d = (s + k) % N_SEQ
        now_copy(s, d).wait_send()
        prev_copy(s, d).wait_send()
        return 0

    lax.fori_loop(1, N_SEQ, drain, 0)
    for side in range(2):
        for i in range(ZA):
            zfar_copy(side, i).wait_send()
        xfar_copy(side).wait_send()
        for g in range(NZ):
            znear_copy(side, g, 0).wait_send()
            znear_copy(side, g, 1).wait_send()
        for half in range(2):
            xnear_copy(side, half).wait_send()
    for part_of in range(3):
        xr_copy(part_of).wait_send()
    for g in range(NZ):
        zx_copy(g).wait_send()
    core_copy.wait_send()
    rdma(stage, dec_ref.at[:, 1 - core], core_sem.at[0], core_sem.at[1], mate).wait_recv()


def body(
    queries, new_kv, cache_now, cache_prev, out_weight, residual, cached_len, new_len, page_table, dest_group
):
    any_spec = pl.BlockSpec(memory_space=pl.ANY)
    dma = pltpu.SemaphoreType.DMA
    vm = pltpu.VMEM
    mixed, decoded = pl.pallas_call(
        kernel,
        out_shape=(
            jax.ShapeDtypeStruct((64, WIDTH), BF),
            jax.ShapeDtypeStruct((4, 2, 8, PAGE, HD), BF),
        ),
        in_specs=[pl.BlockSpec(memory_space=pltpu.SMEM)] * 4 + [any_spec] * 6,
        out_specs=(pl.BlockSpec(memory_space=pltpu.VMEM), pl.BlockSpec(memory_space=pltpu.VMEM)),
        scratch_shapes=[
            vm((FRESH, HEADS * HD), BF),
            vm((2, FRESH, HD), BF),
            vm((2, 16, PAGE, HD), BF),
            vm((4, 16, PAGE, HD), BF),
            vm((HEADS * HD, WIDTH), BF),
            vm((64, WIDTH), BF),
            vm((16, 2, PAGE, HD), BF),
            vm((16, 2, PAGE, HD), BF),
            vm((16, 4, PAGE, HD), BF),
            vm((16, 4, PAGE, HD), BF),
            vm((4, 8, PAGE, HD), BF),
            vm((KEYS, 2 * HD), BF),
            vm((KEYS, 2 * HD), BF),
            vm((HEADS * PAGE, 2 * HD), BF),
            vm((HEADS * PAGE, KEYS), F32),
            vm((PAGE, HEADS * HD), BF),
            vm((4, GROUPS, PAGE, GW), BF),
            vm((3, NX, 64, GW), BF),
            vm((2, ZA, PAGE, GW), BF),
            vm((2, NZ, PAGE, GW), BF),
            vm((2, NX, 64, GW), BF),
            vm((NX, PAGE, GW), BF),
            vm((2, XB, 64, GW), BF),
            vm((2, NX, 64, GW), BF),
            vm((NZ, 64, GW), BF),
            vm((NZ, 64, GW), BF),
            dma((6,)),
            dma((16,)), dma((16,)), dma((16,)), dma((16,)), dma((2,)),
            dma((NZ,)), dma((NZ,)), dma((4 * NZ,)), dma((4 * NZ,)), dma((3,)), dma((3,)),
            dma((2,)), dma((2,)), dma((4,)), dma((4,)), dma((NZ,)), dma((NZ,)),
        ],
        compiler_params=pltpu.CompilerParams(
            collective_id=0, has_side_effects=True, vmem_limit_bytes=66_000_000
        ),
        name="prefill",
    )(
        cached_len,
        new_len,
        page_table,
        dest_group,
        queries,
        new_kv,
        cache_now.reshape(2, 16, PAGE, HD),
        cache_prev.reshape(4, 16, PAGE, HD),
        out_weight,
        residual,
    )
    return mixed, decoded.reshape(2, 2, 2048, HD)


def solution(mesh):
    placed = (
        P("seq", "tp"),
        P(None, "seq", "tp"),
        P(None, "seq", "tp"),
        P(None, None, "seq", "tp"),
        P("tp", None),
        P(("seq", "tp"), None),
        P(),
        P(),
        P(),
        P(),
    )
    return jax.shard_map(
        body,
        mesh=mesh,
        in_specs=placed,
        out_specs=(P(("seq", "tp"), None), P(None, None, "seq", "tp")),
        check_vma=False,
    )
```
